128 devices in a mesh: row: 8 (over x, z_lo), col: 16 (over z_hi, y, core).
Axes of the slice: x: 4, y: 4, z: 4 (z_hi: 2, z_lo: 2; z = z_hi * 2 + z_lo), core: 2. Of those that a mesh axis runs over, the one named last changes fastest.
Arguments:
- upper_tiles: bfloat16 [1024, 5, 256, 256], P('row', None, 'col'), may hold values from -0.8984375 to 0.8984375
- occupied: int32 [1024, 4], P(('row', 'col')), may hold values from 0 to 1, as said below
Outputs:
- square_tiles: bfloat16 [1024, 5, 256, 256], P('row', None, 'col')
The draws below stay inside these ranges and needn't reach their ends.
Inputs may be any that keep to these rules, and one draw needn't show every extreme that they name: Occupancy; its density differs between aligned groups of 8 block rows, and the diagonal block is always occupied (not listed).
All inputs are finite; a program needn't handle non-finite values.
Results may differ from the reference program's by a relative error of at most 0.0024.
Values may be sent and summed in bfloat16 or wider, within the bound.
No kernel may reach another device: no remote copies, remote signals or barrier semaphores. Data moves between devices by JAX's collectives and lax.ppermute only.
A program may use at most 256 MiB of HBM per device.

```python
import jax
import jax.numpy as jnp
from jax import lax

BLOCK = 256
BAND = 4
R_DEV = 8
NB = 1024


def draw_occupied(key, part):
    level_key = jax.random.fold_in(key, 11)
    cell_key = jax.random.fold_in(key, 23)
    levels = jax.random.randint(level_key, (NB // R_DEV, 1), 1, 10)
    levels = jnp.repeat(levels, R_DEV, axis=0)
    cells = jax.random.randint(cell_key, (NB, BAND), 0, 10)
    return (cells < levels).astype(jnp.int32)


def steps_of(stream_key, extent, split, smallest, high):
    factor_of, own = 1.0, jax.random.fold_in(stream_key, 6)
    for dim, blocks in split:
        steps = jnp.exp(jax.random.uniform(jax.random.fold_in(own, dim), (blocks,), jnp.float32, smallest / len(split), high / len(split)))
        factor_of = factor_of * jnp.repeat(steps, extent[dim] // blocks).reshape([-1 if axis == dim else 1 for axis in range(len(extent))])
    return factor_of


def noise(stream_key, shape, spread, bound, shards=(), kind=jnp.bfloat16):
    values = spread * jax.random.normal(stream_key, shape, jnp.float32)
    if shards:
        values = values * steps_of(stream_key, shape, shards, -0.22, 0.18)
    return jnp.clip(values, -bound, bound).astype(kind)


def setup_inputs(seed: int = 0) -> dict:
    key_of = jax.random.split(jax.random.key(seed), 3)
    upper_tiles = noise(key_of[0], (NB, BAND + 1, BLOCK, BLOCK), 0.15, 0.8984375, ((0, 8), (2, 16)))
    occupied = draw_occupied(jax.random.fold_in(key_of[2], 71), 0)
    return dict(upper_tiles=upper_tiles, occupied=occupied)


def build_band(upper_tiles, occupied, first_row, total_rows):
    block_rows = occupied.shape[0]
    band_width = occupied.shape[1]
    row_index = first_row + jnp.arange(block_rows, dtype=jnp.int32)
    offsets = jnp.arange(1, band_width + 1, dtype=jnp.int32)
    kept_mask = (occupied == 1) & (row_index[:, None] + offsets[None, :] < total_rows)
    diag_full = upper_tiles[:, 0].astype(jnp.float32)
    diag_tile = (0.5 * (diag_full + jnp.swapaxes(diag_full, 1, 2))).astype(jnp.bfloat16)
    off_tiles = jnp.where(kept_mask[:, :, None, None], upper_tiles[:, 1:], jnp.zeros((), jnp.bfloat16))
    return jnp.concatenate([diag_tile[:, None], off_tiles], axis=1), kept_mask


def square_band(extended, kept_mask, block_rows, band_width):
    results = []
    for column_shift in range(band_width + 1):
        lefts = []
        rights = []
        for inner in range(column_shift - band_width, band_width + 1):
            start = band_width + inner
            if inner >= 0:
                left = extended[band_width:band_width + block_rows, inner]
            else:
                left = jnp.swapaxes(extended[start:start + block_rows, -inner], 1, 2)
            rest = column_shift - inner
            if rest >= 0:
                right = extended[start:start + block_rows, rest]
            else:
                lower = band_width + column_shift
                right = jnp.swapaxes(extended[lower:lower + block_rows, -rest], 1, 2)
            lefts.append(left)
            rights.append(right)
        left_stack = jnp.stack(lefts, axis=1).astype(jnp.float32)
        right_stack = jnp.stack(rights, axis=1).astype(jnp.float32)
        summed = jnp.einsum("rkab,rkbc->rac", left_stack, right_stack)
        if column_shift > 0:
            summed = jnp.where(kept_mask[:, column_shift - 1, None, None], summed, jnp.zeros((), jnp.float32))
        results.append(summed.astype(jnp.bfloat16))
    return jnp.stack(results, axis=1)


def reference(upper_tiles, occupied):
    groups = NB // R_DEV
    window = R_DEV + 2 * BAND

    def one_group(group):
        first = group * R_DEV - BAND
        rows = first + jnp.arange(window, dtype=jnp.int32)
        valid = (rows >= 0) & (rows < NB)
        index = jnp.clip(rows, 0, NB - 1).astype(jnp.int32)
        tiles = upper_tiles[index]
        occ = occupied[index]
        band, kept_mask = build_band(tiles, occ, first, NB)
        band = jnp.where(valid[:, None, None, None], band, jnp.zeros((), band.dtype))
        return square_band(band, kept_mask[BAND:BAND + R_DEV], R_DEV, BAND)

    stacked = lax.map(one_group, jnp.arange(groups, dtype=jnp.int32))
    return stacked.reshape((NB,) + stacked.shape[2:])
```

```python
import jax
import jax.numpy as jnp
from jax import lax
from jax.experimental import pallas as pl
from jax.experimental.pallas import tpu as pltpu
from jax.sharding import PartitionSpec as P

AXES = ("row", "col")
BLOCK = 256
BAND = 4
LANES = (2 * BAND + 1) * BLOCK
BELOW = [(m, d) for m in range(1, BAND + 1) for d in range(m, BAND + 1)]
ABOVE = [(m, d) for m in range(BAND) for d in range(BAND - m)]


def halo_kernel(tiles, to_next, to_last, sem):
    rows = tiles.shape[1]
    copies = []
    start = 0
    for m in range(1, BAND + 1):
        count = BAND + 1 - m
        copies.append(
            (tiles.at[:, rows - m, pl.ds(m, count)], to_next.at[:, pl.ds(start, count)])
        )
        start += count
    start = 0
    for m in range(BAND):
        count = BAND - m
        copies.append((tiles.at[:, m, pl.ds(0, count)], to_last.at[:, pl.ds(start, count)]))
        start += count
    started = [
        pltpu.make_async_copy(source, target, sem.at[n])
        for n, (source, target) in enumerate(copies)
    ]
    for copy in started:
        copy.start()
    for copy in started:
        copy.wait()


def halo_tiles(tiles):
    parts, _, _, height, width = tiles.shape
    anywhere = pl.BlockSpec(memory_space=pl.ANY)
    shape = jax.ShapeDtypeStruct((parts, len(BELOW), height, width), tiles.dtype)
    return pl.pallas_call(
        halo_kernel,
        out_shape=(shape, shape),
        in_specs=[anywhere],
        out_specs=(anywhere, anywhere),
        scratch_shapes=[pltpu.SemaphoreType.DMA((2 * BAND,))],
    )(tiles)


def square_kernel(kept, kept_below, kept_above, tiles, below, above, out, strips, done, sem, out_sem):
    rows = tiles.shape[1]
    parts, height = tiles.shape[0], tiles.shape[3]

    def offsets(row):
        if row < 0:
            return [d for m, d in BELOW if m == -row]
        if row >= rows:
            return [d for m, d in ABOVE if m == row - rows]
        return list(range(BAND + 1))

    def stored(row, d):
        if row < 0:
            return below.at[:, BELOW.index((-row, d))]
        if row >= rows:
            return above.at[:, ABOVE.index((row - rows, d))]
        return tiles.at[:, row, d]

    def flag(row, d):
        if row < 0:
            return kept_below[BAND + row, d - 1]
        if row >= rows:
            return kept_above[row - rows, d - 1]
        return kept[row, d - 1]

    def block(row, d):
        return strips.at[BAND + row, :, :, pl.ds((BAND + d) * BLOCK, BLOCK)]

    def load(row, d):
        return pltpu.make_async_copy(stored(row, d), block(row, d), sem.at[BAND + row, d])

    def get(row, d):
        return block(row, d)[...].reshape(BLOCK, BLOCK)

    def put(row, d, value):
        block(row, d)[...] = value.reshape(parts, height, BLOCK)

    for row in range(-BAND, rows + BAND):
        for d in offsets(row):
            load(row, d).start()

    ready = set()

    def arrive(row):
        if row in ready:
            return
        ready.add(row)
        for d in offsets(row):
            load(row, d).wait()
            if d > 0:

                @pl.when(flag(row, d) == 0)
                def _():
                    put(row, d, jnp.zeros((BLOCK, BLOCK), jnp.bfloat16))

    def prepare(j):
        for k in range(j - BAND, j + 1):
            arrive(k)
        raw = get(j, 0)
        both = raw.astype(jnp.float32) + raw.T.astype(jnp.float32)
        put(j, 0, (0.5 * both).astype(jnp.bfloat16))
        for m in range(1, BAND + 1):
            put(j, -m, get(j - m, m).T)

    def store(i, e):
        return pltpu.make_async_copy(done.at[i, e], out.at[:, i, e], out_sem)

    for j in range(BAND):
        prepare(j)
    for i in range(rows):
        prepare(i + BAND)
        for e in range(BAND + 1):
            depth = LANES - e * BLOCK
            left = strips[BAND + i, :, :, pl.ds(e * BLOCK, depth)].reshape(BLOCK, depth)
            right = strips[BAND + i + e, :, :, pl.ds(0, depth)].reshape(BLOCK, depth)
            summed = lax.dot_general(
                left, right, (((1,), (1,)), ((), ())), preferred_element_type=jnp.float32
            )
            if e > 0:
                summed = jnp.where(kept[i, e - 1] != 0, summed, 0.0)
            done[i, e] = summed.astype(jnp.bfloat16).reshape(parts, height, BLOCK)
            store(i, e).start()
    for i in range(rows):
        for e in range(BAND + 1):
            store(i, e).wait()


def square_band(kept, kept_below, kept_above, tiles, below, above):
    parts, rows, width, height, _ = tiles.shape
    scalars = pl.BlockSpec(memory_space=pltpu.SMEM)
    anywhere = pl.BlockSpec(memory_space=pl.ANY)
    return pl.pallas_call(
        square_kernel,
        out_shape=jax.ShapeDtypeStruct(tiles.shape, jnp.bfloat16),
        in_specs=[scalars] * 3 + [anywhere] * 3,
        out_specs=anywhere,
        scratch_shapes=[
            pltpu.VMEM((rows + 2 * BAND, parts, height, LANES), jnp.bfloat16),
            pltpu.VMEM((rows, width, parts, height, BLOCK), jnp.bfloat16),
            pltpu.SemaphoreType.DMA((rows + 2 * BAND, width)),
            pltpu.SemaphoreType.DMA,
        ],
        compiler_params=pltpu.CompilerParams(vmem_limit_bytes=48 << 20),
    )(kept, kept_below, kept_above, tiles, below, above)


def shards(upper_tiles, occupied):
    parts = lax.axis_size("col")
    count = lax.axis_size("row") * parts
    rows, band = occupied.shape
    position = lax.axis_index("row") * parts + lax.axis_index("col")
    index = position * rows + jnp.arange(rows, dtype=jnp.int32)
    offsets = jnp.arange(1, band + 1, dtype=jnp.int32)
    inside = index[:, None] + offsets[None, :] < rows * count
    kept = ((occupied == 1) & inside).astype(jnp.int32)
    forward = [(p, p + 1) for p in range(count - 1)]
    backward = [(p + 1, p) for p in range(count - 1)]
    kept_below = lax.ppermute(kept[rows - BAND :], AXES, forward)
    kept_above = lax.ppermute(kept[:BAND], AXES, backward)
    tiles = upper_tiles.reshape((parts, rows) + upper_tiles.shape[1:])
    tiles = lax.all_to_all(tiles, "col", 0, 0, tiled=True)
    to_next, to_last = halo_tiles(tiles)
    below = lax.ppermute(to_next, AXES, forward)
    above = lax.ppermute(to_last, AXES, backward)
    product = square_band(kept, kept_below, kept_above, tiles, below, above)
    product = lax.all_to_all(product, "col", 0, 0, tiled=True)
    return product.reshape(upper_tiles.shape)


def solution(mesh):
    return jax.shard_map(
        shards,
        mesh=mesh,
        in_specs=(P("row", None, "col", None), P(("row", "col"), None)),
        out_specs=P("row", None, "col", None),
        check_vma=False,
    )
```

```python
import jax
import jax.numpy as jnp
from jax import lax
from jax.experimental import pallas as pl
from jax.experimental.pallas import tpu as pltpu
from jax.sharding import PartitionSpec as P

AXES = ("row", "col")
BLOCK = 256
BAND = 4
LANES = (2 * BAND + 1) * BLOCK
BELOW = [(m, d) for m in range(1, BAND + 1) for d in range(m, BAND + 1)]
ABOVE = [(m, d) for m in range(BAND) for d in range(BAND - m)]

SCALARS = pl.BlockSpec(memory_space=pltpu.SMEM)
ANYWHERE = pl.BlockSpec(memory_space=pl.ANY)
ONCHIP = pl.BlockSpec(memory_space=pltpu.VMEM)


def partial_tiles(rows):
    return [
        (i, e) for i in range(rows) for e in range(BAND + 1) if i + e < BAND or i + e >= rows
    ]


def times_transposed(left, right):
    return lax.dot_general(
        left, right, (((1,), (1,)), ((), ())), preferred_element_type=jnp.float32
    )


def symmetric(raw):
    both = raw.astype(jnp.float32) + raw.T.astype(jnp.float32)
    return (0.5 * both).astype(jnp.bfloat16)


def limit(mebibytes):
    return pltpu.CompilerParams(vmem_limit_bytes=mebibytes << 20)


def onchip(array):
    return pltpu.with_memory_space_constraint(array, pltpu.VMEM)


def halo_kernel(kept, tiles, to_next, to_last, sem):
    rows = tiles.shape[1]
    copies = []
    start = 0
    for m in range(1, BAND + 1):
        count = BAND + 1 - m
        copies.append(
            (tiles.at[:, rows - m, pl.ds(m, count)], to_next.at[:, pl.ds(start, count)])
        )
        start += count
    start = 0
    for m in range(BAND):
        count = BAND - m
        copies.append((tiles.at[:, m, pl.ds(0, count)], to_last.at[:, pl.ds(start, count)]))
        start += count
    started = [
        pltpu.make_async_copy(source, target, sem.at[n])
        for n, (source, target) in enumerate(copies)
    ]
    for copy in started:
        copy.start()
    for copy in started:
        copy.wait()

    def mask(row, d, target, slot):
        if d > 0:

            @pl.when(kept[row, d - 1] == 0)
            def _():
                target[:, slot] = jnp.zeros_like(target[:, slot])

    for slot, (m, d) in enumerate(BELOW):
        mask(rows - m, d, to_next, slot)
    for slot, (m, d) in enumerate(ABOVE):
        mask(m, d, to_last, slot)


def halo_tiles(kept, tiles):
    parts, _, _, height, width = tiles.shape
    shape = pltpu.VMEM((parts, len(BELOW), height, width), tiles.dtype)
    return pl.pallas_call(
        halo_kernel,
        out_shape=(shape, shape),
        in_specs=[SCALARS, ANYWHERE],
        out_specs=(ONCHIP, ONCHIP),
        scratch_shapes=[pltpu.SemaphoreType.DMA((2 * BAND,))],
        compiler_params=limit(4),
    )(kept, tiles)


def local_kernel(kept, tiles, out, partial, strips, done, sem, out_sem):
    parts, rows, _, height, _ = tiles.shape
    waiting = partial_tiles(rows)

    def block(row, d):
        return strips.at[row, :, :, pl.ds((BAND + d) * BLOCK, BLOCK)]

    def load(row, d):
        return pltpu.make_async_copy(tiles.at[:, row, d], block(row, d), sem.at[row, d])

    def get(row, d):
        return block(row, d)[...].reshape(BLOCK, BLOCK)

    def put(row, d, value):
        block(row, d)[...] = value.reshape(parts, height, BLOCK)

    def store(i, e):
        return pltpu.make_async_copy(done.at[i, e], out.at[:, i, e], out_sem)

    for row in range(rows):
        for d in range(BAND + 1):
            load(row, d).start()

    def arrive(row):
        for d in range(BAND + 1):
            load(row, d).wait()
            if d > 0:

                @pl.when(kept[row, d - 1] == 0)
                def _():
                    put(row, d, jnp.zeros((BLOCK, BLOCK), jnp.bfloat16))

    def prepare(j):
        if j < rows:
            arrive(j)
            put(j, 0, symmetric(get(j, 0)))
        for m in range(1, BAND + 1):
            if 0 <= j - m < rows:
                put(j, -m, get(j - m, m).T)

    for j in range(BAND):
        prepare(j)
    for i in range(rows):
        prepare(i + BAND)
        for e in range(BAND + 1):
            j = i + e
            first = max(0, j - BAND)
            last = i + BAND if j < rows else rows - 1
            depth = (last + 1 - first) * BLOCK
            left = strips[i, :, :, pl.ds((first - i + BAND) * BLOCK, depth)]
            right = strips[j, :, :, pl.ds((first - j + BAND) * BLOCK, depth)]
            summed = times_transposed(left.reshape(BLOCK, depth), right.reshape(BLOCK, depth))
            if (i, e) in waiting:
                partial[waiting.index((i, e))] = summed
            else:
                if e > 0:
                    summed = jnp.where(kept[i, e - 1] != 0, summed, 0.0)
                done[i, e] = summed.astype(jnp.bfloat16).reshape(parts, height, BLOCK)
                store(i, e).start()
    for i in range(rows):
        for e in range(BAND + 1):
            if (i, e) not in waiting:
                store(i, e).wait()


def square_local(kept, tiles):
    parts, rows, width, height, _ = tiles.shape
    count = len(partial_tiles(rows))
    return pl.pallas_call(
        local_kernel,
        out_shape=(
            jax.ShapeDtypeStruct(tiles.shape, jnp.bfloat16),
            pltpu.VMEM((count, BLOCK, BLOCK), jnp.float32),
        ),
        in_specs=[SCALARS, ANYWHERE],
        out_specs=(ANYWHERE, ONCHIP),
        scratch_shapes=[
            pltpu.VMEM((rows + BAND, parts, height, LANES), jnp.bfloat16),
            pltpu.VMEM((rows, width, parts, height, BLOCK), jnp.bfloat16),
            pltpu.SemaphoreType.DMA((rows, width)),
            pltpu.SemaphoreType.DMA,
        ],
        compiler_params=limit(30),
    )(kept, tiles)


def border_kernel(kept, to_next, below, above, partial, _, out, done, out_sem):
    parts, rows, _, height, _ = out.shape
    waiting = partial_tiles(rows)

    def get(ref, slot):
        return ref[:, slot].reshape(BLOCK, BLOCK)

    def store(slot):
        i, e = waiting[slot]
        return pltpu.make_async_copy(done.at[slot], out.at[:, i, e], out_sem)

    def finish(i, e, summed):
        slot = waiting.index((i, e))
        summed = partial[slot] + summed
        if e > 0:
            summed = jnp.where(kept[i, e - 1] != 0, summed, 0.0)
        done[slot] = summed.astype(jnp.bfloat16).reshape(parts, height, BLOCK)
        store(slot).start()

    lower = {
        j: jnp.concatenate(
            [get(below, BELOW.index((m, j + m))).T for m in range(BAND - j, 0, -1)], axis=1
        )
        for j in range(BAND)
    }
    for j in range(BAND):
        depth = (BAND - j) * BLOCK
        for i in range(j + 1):
            left = lower[i][:, lower[i].shape[1] - depth :]
            finish(i, j - i, times_transposed(left, lower[j]))

    def corner(a, b):
        if a == b:
            return symmetric(get(above, ABOVE.index((a, 0))))
        if a < b:
            return get(above, ABOVE.index((a, b - a)))
        return get(above, ABOVE.index((b, a - b))).T

    square = [
        jnp.concatenate([corner(a, b) for b in range(BAND)], axis=1) for a in range(BAND)
    ]
    for i in range(rows - BAND, rows):
        reach = i + BAND + 1 - rows
        left = jnp.concatenate(
            [get(to_next, BELOW.index((rows - i, rows + b - i))) for b in range(reach)], axis=1
        )
        for a in range(reach):
            finish(i, rows + a - i, times_transposed(left, square[a][:, : reach * BLOCK]))
    for slot in range(len(waiting)):
        store(slot).wait()


def square_border(kept, to_next, below, above, partial, product):
    parts, rows, _, height, _ = product.shape
    return pl.pallas_call(
        border_kernel,
        out_shape=jax.ShapeDtypeStruct(product.shape, product.dtype),
        in_specs=[SCALARS, ONCHIP, ONCHIP, ONCHIP, ONCHIP, ANYWHERE],
        out_specs=ANYWHERE,
        scratch_shapes=[
            pltpu.VMEM((partial.shape[0], parts, height, BLOCK), jnp.bfloat16),
            pltpu.SemaphoreType.DMA,
        ],
        input_output_aliases={5: 0},
        compiler_params=limit(20),
    )(kept, *(onchip(a) for a in (to_next, below, above, partial)), product)


def shards(upper_tiles, occupied):
    parts = lax.axis_size("col")
    count = lax.axis_size("row") * parts
    rows, band = occupied.shape
    position = lax.axis_index("row") * parts + lax.axis_index("col")
    index = position * rows + jnp.arange(rows, dtype=jnp.int32)
    offsets = jnp.arange(1, band + 1, dtype=jnp.int32)
    inside = index[:, None] + offsets[None, :] < rows * count
    kept = ((occupied == 1) & inside).astype(jnp.int32)
    tiles = upper_tiles.reshape((parts, rows) + upper_tiles.shape[1:])
    tiles = lax.all_to_all(tiles, "col", 0, 0, tiled=True)
    to_next, to_last = halo_tiles(kept, tiles)
    below = lax.ppermute(to_next, AXES, [(p, p + 1) for p in range(count - 1)])
    above = lax.ppermute(to_last, AXES, [(p + 1, p) for p in range(count - 1)])
    product, partial = square_local(kept, tiles)
    product = square_border(kept, to_next, below, above, partial, product)
    product = lax.all_to_all(product, "col", 0, 0, tiled=True)
    return product.reshape(upper_tiles.shape)


def solution(mesh):
    return jax.shard_map(
        shards,
        mesh=mesh,
        in_specs=(P("row", None, "col", None), P(("row", "col"), None)),
        out_specs=P("row", None, "col", None),
        check_vma=False,
    )
```

```python
import jax
import jax.numpy as jnp
from jax import lax
from jax.experimental import pallas as pl
from jax.experimental.pallas import tpu as pltpu
from jax.sharding import PartitionSpec as P

AXES = ("row", "col")
BLOCK = 256
BAND = 4
LANES = (2 * BAND + 1) * BLOCK
BELOW = [(m, d) for m in range(1, BAND + 1) for d in range(m, BAND + 1)]
ABOVE = [(m, d) for m in range(BAND) for d in range(BAND - m)]

SCALARS = pl.BlockSpec(memory_space=pltpu.SMEM)
ANYWHERE = pl.BlockSpec(memory_space=pl.ANY)
ONCHIP = pl.BlockSpec(memory_space=pltpu.VMEM)


def partial_tiles(rows):
    return [
        (i, e) for i in range(rows) for e in range(BAND + 1) if i + e < BAND or i + e >= rows
    ]


def keep(occupied, row, d):
    rows = occupied.shape[0]
    here = lax.axis_index("row") * lax.axis_size("col") + lax.axis_index("col")
    there = lax.axis_size("row") * lax.axis_size("col")
    return (occupied[row, d - 1] == 1) & (here * rows + row + d < there * rows)


def times_transposed(left, right):
    return lax.dot_general(
        left, right, (((1,), (1,)), ((), ())), preferred_element_type=jnp.float32
    )


def symmetric(raw):
    both = raw.astype(jnp.float32) + raw.T.astype(jnp.float32)
    return (0.5 * both).astype(jnp.bfloat16)


def limit(mebibytes):
    return pltpu.CompilerParams(vmem_limit_bytes=mebibytes << 20)


def onchip(array):
    return pltpu.with_memory_space_constraint(array, pltpu.VMEM)


def halo_kernel(occupied, tiles, to_next, to_last, sem):
    rows = tiles.shape[1]
    copies = []
    start = 0
    for m in range(1, BAND + 1):
        count = BAND + 1 - m
        copies.append(
            (tiles.at[:, rows - m, pl.ds(m, count)], to_next.at[:, pl.ds(start, count)])
        )
        start += count
    start = 0
    for m in range(BAND):
        count = BAND - m
        copies.append((tiles.at[:, m, pl.ds(0, count)], to_last.at[:, pl.ds(start, count)]))
        start += count
    started = [
        pltpu.make_async_copy(source, target, sem.at[n])
        for n, (source, target) in enumerate(copies)
    ]
    for copy in started:
        copy.start()
    for copy in started:
        copy.wait()

    def mask(row, d, target, slot):
        if d > 0:

            @pl.when(jnp.logical_not(keep(occupied, row, d)))
            def _():
                target[:, slot] = jnp.zeros_like(target[:, slot])

    for slot, (m, d) in enumerate(BELOW):
        mask(rows - m, d, to_next, slot)
    for slot, (m, d) in enumerate(ABOVE):
        mask(m, d, to_last, slot)


def halo_tiles(occupied, tiles):
    parts, _, _, height, width = tiles.shape
    shape = pltpu.VMEM((parts, len(BELOW), height, width), tiles.dtype)
    return pl.pallas_call(
        halo_kernel,
        out_shape=(shape, shape),
        in_specs=[SCALARS, ANYWHERE],
        out_specs=(ONCHIP, ONCHIP),
        scratch_shapes=[pltpu.SemaphoreType.DMA((2 * BAND,))],
        compiler_params=limit(4),
    )(occupied, tiles)


def local_kernel(occupied, tiles, out, partial, strips, sem):
    parts, rows, _, height, _ = tiles.shape
    waiting = partial_tiles(rows)

    def block(row, d):
        return strips.at[row, :, :, pl.ds((BAND + d) * BLOCK, BLOCK)]

    def load(row, d):
        return pltpu.make_async_copy(tiles.at[:, row, d], block(row, d), sem.at[row, d])

    def get(row, d):
        return block(row, d)[...].reshape(BLOCK, BLOCK)

    def put(row, d, value):
        block(row, d)[...] = value.reshape(parts, height, BLOCK)

    for row in range(rows):
        for d in range(BAND + 1):
            load(row, d).start()

    def arrive(row):
        for d in range(BAND + 1):
            load(row, d).wait()
            if d > 0:

                @pl.when(jnp.logical_not(keep(occupied, row, d)))
                def _():
                    put(row, d, jnp.zeros((BLOCK, BLOCK), jnp.bfloat16))

    def prepare(j):
        if j < rows:
            arrive(j)
            put(j, 0, symmetric(get(j, 0)))
        for m in range(1, BAND + 1):
            if 0 <= j - m < rows:
                put(j, -m, get(j - m, m).T)

    for j in range(BAND):
        prepare(j)
    for i in range(rows):
        prepare(i + BAND)
        for e in range(BAND + 1):
            j = i + e
            first = max(0, j - BAND)
            last = i + BAND if j < rows else rows - 1
            depth = (last + 1 - first) * BLOCK
            rows_i = strips[i, :, :, pl.ds((first - i + BAND) * BLOCK, depth)]
            rows_j = strips[j, :, :, pl.ds((first - j + BAND) * BLOCK, depth)]
            summed = times_transposed(rows_i.reshape(BLOCK, depth), rows_j.reshape(BLOCK, depth))
            if (i, e) in waiting:
                partial[waiting.index((i, e))] = summed
            else:
                if e > 0:
                    summed = jnp.where(keep(occupied, i, e), summed, 0.0)
                out[:, i, e] = summed.astype(jnp.bfloat16).reshape(parts, height, BLOCK)


def square_local(occupied, tiles):
    parts, rows, width, height, _ = tiles.shape
    count = len(partial_tiles(rows))
    return pl.pallas_call(
        local_kernel,
        out_shape=(
            pltpu.VMEM(tiles.shape, jnp.bfloat16),
            pltpu.VMEM((count, BLOCK, BLOCK), jnp.float32),
        ),
        in_specs=[SCALARS, ANYWHERE],
        out_specs=(ONCHIP, ONCHIP),
        scratch_shapes=[
            pltpu.VMEM((rows + BAND, parts, height, LANES), jnp.bfloat16),
            pltpu.SemaphoreType.DMA((rows, width)),
        ],
        compiler_params=limit(30),
    )(occupied, tiles)


def border_kernel(occupied, to_next, below, above, partial, _, out):
    parts, rows, _, height, _ = out.shape
    waiting = partial_tiles(rows)

    def get(ref, slot):
        return ref[:, slot].reshape(BLOCK, BLOCK)

    def finish(i, e, summed):
        slot = waiting.index((i, e))
        summed = partial[slot] + summed
        if e > 0:
            summed = jnp.where(keep(occupied, i, e), summed, 0.0)
        out[:, i, e] = summed.astype(jnp.bfloat16).reshape(parts, height, BLOCK)

    lower = {
        j: jnp.concatenate(
            [get(below, BELOW.index((m, j + m))).T for m in range(BAND - j, 0, -1)], axis=1
        )
        for j in range(BAND)
    }
    for j in range(BAND):
        depth = (BAND - j) * BLOCK
        for i in range(j + 1):
            rows_i = lower[i][:, lower[i].shape[1] - depth :]
            finish(i, j - i, times_transposed(rows_i, lower[j]))

    def corner(a, b):
        if a == b:
            return symmetric(get(above, ABOVE.index((a, 0))))
        if a < b:
            return get(above, ABOVE.index((a, b - a)))
        return get(above, ABOVE.index((b, a - b))).T

    square = [
        jnp.concatenate([corner(a, b) for b in range(BAND)], axis=1) for a in range(BAND)
    ]
    for i in range(rows - BAND, rows):
        reach = i + BAND + 1 - rows
        rows_i = jnp.concatenate(
            [get(to_next, BELOW.index((rows - i, rows + b - i))) for b in range(reach)], axis=1
        )
        for a in range(reach):
            finish(i, rows + a - i, times_transposed(rows_i, square[a][:, : reach * BLOCK]))


def square_border(occupied, to_next, below, above, partial, product):
    return pl.pallas_call(
        border_kernel,
        out_shape=pltpu.VMEM(product.shape, product.dtype),
        in_specs=[SCALARS] + [ONCHIP] * 5,
        out_specs=ONCHIP,
        input_output_aliases={5: 0},
        compiler_params=limit(20),
    )(occupied, *(onchip(a) for a in (to_next, below, above, partial, product)))


def shards(upper_tiles, occupied):
    parts = lax.axis_size("col")
    count = lax.axis_size("row") * parts
    rows = occupied.shape[0]
    tiles = upper_tiles.reshape((parts, rows) + upper_tiles.shape[1:])
    tiles = lax.all_to_all(tiles, "col", 0, 0, tiled=True)
    tiles, occupied = lax.optimization_barrier((tiles, occupied))
    to_next, to_last = halo_tiles(occupied, tiles)
    below = lax.ppermute(to_next, AXES, [(p, p + 1) for p in range(count - 1)])
    above = lax.ppermute(to_last, AXES, [(p + 1, p) for p in range(count - 1)])
    product, partial = square_local(occupied, tiles)
    product = square_border(occupied, to_next, below, above, partial, product)
    product = lax.all_to_all(product, "col", 0, 0, tiled=True)
    return product.reshape(upper_tiles.shape)


def solution(mesh):
    return jax.shard_map(
        shards,
        mesh=mesh,
        in_specs=(P("row", None, "col", None), P(("row", "col"), None)),
        out_specs=P("row", None, "col", None),
        check_vma=False,
    )
```

```python
import jax
import jax.numpy as jnp
from jax import lax
from jax.experimental import pallas as pl
from jax.experimental.pallas import tpu as pltpu
from jax.sharding import PartitionSpec as P

AXES = ("row", "col")
BLOCK = 256
BAND = 4
LANES = (2 * BAND + 1) * BLOCK
BELOW = [(m, d) for m in range(1, BAND + 1) for d in range(m, BAND + 1)]
ABOVE = [(m, d) for m in range(BAND) for d in range(BAND - m)]

SCALARS = pl.BlockSpec(memory_space=pltpu.SMEM)
OFFCHIP = pl.BlockSpec(memory_space=pltpu.HBM)
ONCHIP = pl.BlockSpec(memory_space=pltpu.VMEM)


def partial_tiles(rows):
    return [
        (i, e) for i in range(rows) for e in range(BAND + 1) if i + e < BAND or i + e >= rows
    ]


def keep(occupied, row, d):
    rows = occupied.shape[0]
    here = lax.axis_index("row") * lax.axis_size("col") + lax.axis_index("col")
    there = lax.axis_size("row") * lax.axis_size("col")
    return (occupied[row, d - 1] == 1) & (here * rows + row + d < there * rows)


def times_transposed(left, right):
    return lax.dot_general(
        left, right, (((1,), (1,)), ((), ())), preferred_element_type=jnp.float32
    )


def symmetric(raw):
    both = raw.astype(jnp.float32) + raw.T.astype(jnp.float32)
    return (0.5 * both).astype(jnp.bfloat16)


def limit(mebibytes):
    return pltpu.CompilerParams(vmem_limit_bytes=mebibytes << 20)


def onchip(array):
    return pltpu.with_memory_space_constraint(array, pltpu.VMEM)


def is_odd():
    return lax.rem(lax.axis_index("col"), 2)


def halo_kernel(occupied, tiles, across, beside, sem):
    rows = tiles.shape[1]
    odd = is_odd()
    copies = []
    spans = []
    start = 0
    for m in range(1, BAND + 1):
        count = BAND + 1 - m
        for target, upward in ((across, odd), (beside, 1 - odd)):
            row = upward * (rows - m) + (1 - upward) * (m - 1)
            first = upward * m
            copies.append(
                pltpu.make_async_copy(
                    tiles.at[:, row, pl.ds(first, count)],
                    target.at[:, pl.ds(start, count)],
                    sem.at[len(copies)],
                )
            )
            spans.append((target, start, count, row, first))
        start += count
    for copy in copies:
        copy.start()
    for copy in copies:
        copy.wait()
    for target, start, count, row, first in spans:
        for step in range(count):
            d = first + step
            dropped = (d > 0) & jnp.logical_not(keep(occupied, row, jnp.maximum(d, 1)))

            @pl.when(dropped)
            def _():
                target[:, start + step] = jnp.zeros_like(target[:, start + step])


def halo_tiles(occupied, tiles):
    parts, _, _, height, width = tiles.shape
    shape = pltpu.VMEM((parts, len(BELOW), height, width), tiles.dtype)
    return pl.pallas_call(
        halo_kernel,
        out_shape=(shape, shape),
        in_specs=[SCALARS, OFFCHIP],
        out_specs=(ONCHIP, ONCHIP),
        scratch_shapes=[pltpu.SemaphoreType.DMA((2 * BAND,))],
        compiler_params=limit(4),
    )(occupied, pltpu.with_memory_space_constraint(tiles, pltpu.HBM))


def local_kernel(occupied, tiles, out, partial, strips, sem):
    parts, rows, _, height, _ = tiles.shape
    waiting = partial_tiles(rows)

    def block(row, d):
        return strips.at[row, :, :, pl.ds((BAND + d) * BLOCK, BLOCK)]

    def load(row, d):
        return pltpu.make_async_copy(tiles.at[:, row, d], block(row, d), sem.at[row, d])

    def get(row, d):
        return block(row, d)[...].reshape(BLOCK, BLOCK)

    def put(row, d, value):
        block(row, d)[...] = value.reshape(parts, height, BLOCK)

    for row in range(rows):
        for d in range(BAND + 1):
            load(row, d).start()

    def arrive(row):
        for d in range(BAND + 1):
            load(row, d).wait()
            if d > 0:

                @pl.when(jnp.logical_not(keep(occupied, row, d)))
                def _():
                    put(row, d, jnp.zeros((BLOCK, BLOCK), jnp.bfloat16))

    def prepare(j):
        if j < rows:
            arrive(j)
            put(j, 0, symmetric(get(j, 0)))
        for m in range(1, BAND + 1):
            if 0 <= j - m < rows:
                put(j, -m, get(j - m, m).T)

    for j in range(BAND):
        prepare(j)
    for i in range(rows):
        prepare(i + BAND)
        for e in range(BAND + 1):
            j = i + e
            first = max(0, j - BAND)
            last = i + BAND if j < rows else rows - 1
            depth = (last + 1 - first) * BLOCK
            rows_i = strips[i, :, :, pl.ds((first - i + BAND) * BLOCK, depth)]
            rows_j = strips[j, :, :, pl.ds((first - j + BAND) * BLOCK, depth)]
            summed = times_transposed(rows_i.reshape(BLOCK, depth), rows_j.reshape(BLOCK, depth))
            if (i, e) in waiting:
                partial[waiting.index((i, e))] = summed
            else:
                if e > 0:
                    summed = jnp.where(keep(occupied, i, e), summed, 0.0)
                out[:, i, e] = summed.astype(jnp.bfloat16).reshape(parts, height, BLOCK)


def square_local(occupied, tiles):
    parts, rows, width, height, _ = tiles.shape
    count = len(partial_tiles(rows))
    return pl.pallas_call(
        local_kernel,
        out_shape=(
            pltpu.VMEM(tiles.shape, jnp.bfloat16),
            pltpu.VMEM((count, BLOCK, BLOCK), jnp.float32),
        ),
        in_specs=[SCALARS, OFFCHIP],
        out_specs=(ONCHIP, ONCHIP),
        scratch_shapes=[
            pltpu.VMEM((rows + BAND, parts, height, LANES), jnp.bfloat16),
            pltpu.SemaphoreType.DMA((rows, width)),
        ],
        compiler_params=limit(30),
    )(occupied, pltpu.with_memory_space_constraint(tiles, pltpu.HBM))


def border_kernel(occupied, sent_across, sent_beside, across, beside, partial, _, out):
    odd = is_odd() == 1
    to_next = (sent_across, sent_beside)
    below = (beside, across)
    above = (across, beside)
    parts, rows, _, height, _ = out.shape
    waiting = partial_tiles(rows)

    def get(refs, slot):
        return jnp.where(odd, refs[0][:, slot], refs[1][:, slot]).reshape(BLOCK, BLOCK)

    def finish(i, e, summed):
        slot = waiting.index((i, e))
        summed = partial[slot] + summed
        if e > 0:
            summed = jnp.where(keep(occupied, i, e), summed, 0.0)
        out[:, i, e] = summed.astype(jnp.bfloat16).reshape(parts, height, BLOCK)

    lower = {
        j: jnp.concatenate(
            [get(below, BELOW.index((m, j + m))).T for m in range(BAND - j, 0, -1)], axis=1
        )
        for j in range(BAND)
    }
    for j in range(BAND):
        depth = (BAND - j) * BLOCK
        for i in range(j + 1):
            rows_i = lower[i][:, lower[i].shape[1] - depth :]
            finish(i, j - i, times_transposed(rows_i, lower[j]))

    def corner(a, b):
        if a == b:
            return symmetric(get(above, ABOVE.index((a, 0))))
        if a < b:
            return get(above, ABOVE.index((a, b - a)))
        return get(above, ABOVE.index((b, a - b))).T

    square = [
        jnp.concatenate([corner(a, b) for b in range(BAND)], axis=1) for a in range(BAND)
    ]
    for i in range(rows - BAND, rows):
        reach = i + BAND + 1 - rows
        rows_i = jnp.concatenate(
            [get(to_next, BELOW.index((rows - i, rows + b - i))) for b in range(reach)], axis=1
        )
        for a in range(reach):
            finish(i, rows + a - i, times_transposed(rows_i, square[a][:, : reach * BLOCK]))


def square_border(occupied, halo, partial, product):
    return pl.pallas_call(
        border_kernel,
        out_shape=pltpu.VMEM(product.shape, product.dtype),
        in_specs=[SCALARS] + [ONCHIP] * 6,
        out_specs=ONCHIP,
        input_output_aliases={6: 0},
        compiler_params=limit(20),
    )(occupied, *(onchip(a) for a in (*halo, partial, product)))


def swaps(firsts):
    return [pair for p in firsts for pair in ((p, p + 1), (p + 1, p))]


def shards(upper_tiles, occupied):
    parts = lax.axis_size("col")
    count = lax.axis_size("row") * parts
    rows = occupied.shape[0]
    tiles = upper_tiles.reshape((parts, rows) + upper_tiles.shape[1:])
    tiles = lax.all_to_all(tiles, "col", 0, 0, tiled=True)
    tiles, occupied = lax.optimization_barrier((tiles, occupied))
    sent_across, sent_beside = halo_tiles(occupied, tiles)
    across = lax.ppermute(sent_across, AXES, swaps(range(1, count - 1, 2)))
    beside = lax.ppermute(sent_beside, AXES, swaps(range(0, count, 2)))
    product, partial = square_local(occupied, tiles)
    halo = (sent_across, sent_beside, across, beside)
    product = square_border(occupied, halo, partial, product)
    product = lax.all_to_all(product, "col", 0, 0, tiled=True)
    return product.reshape(upper_tiles.shape)


def solution(mesh):
    return jax.shard_map(
        shards,
        mesh=mesh,
        in_specs=(P("row", None, "col", None), P(("row", "col"), None)),
        out_specs=P("row", None, "col", None),
        check_vma=False,
    )
```

```python
import functools

import jax
import jax.numpy as jnp
from jax import lax
from jax.experimental import pallas as pl
from jax.experimental.pallas import tpu as pltpu
from jax.sharding import PartitionSpec as P


AXES = ("row", "col")
BLOCK = 256
BAND = 4
LANES = (2 * BAND + 1) * BLOCK
BELOW = [(m, d) for m in range(1, BAND + 1) for d in range(m, BAND + 1)]
ABOVE = [(m, d) for m in range(BAND) for d in range(BAND - m)]

SCALARS = pl.BlockSpec(memory_space=pltpu.SMEM)
OFFCHIP = pl.BlockSpec(memory_space=pltpu.HBM)
ONCHIP = pl.BlockSpec(memory_space=pltpu.VMEM)


def partial_tiles(rows):
    return [
        (i, e) for i in range(rows) for e in range(BAND + 1) if i + e < BAND or i + e >= rows
    ]


def keep(occupied, row, d):
    rows = occupied.shape[0]
    here = lax.axis_index("row") * lax.axis_size("col") + lax.axis_index("col")
    there = lax.axis_size("row") * lax.axis_size("col")
    return (occupied[row, d - 1] == 1) & (here * rows + row + d < there * rows)


def times_transposed(left, right):
    return lax.dot_general(
        left, right, (((1,), (1,)), ((), ())), preferred_element_type=jnp.float32
    )


def symmetric(raw):
    both = raw.astype(jnp.float32) + raw.T.astype(jnp.float32)
    return (0.5 * both).astype(jnp.bfloat16)


def offchip(array):
    return pltpu.with_memory_space_constraint(array, pltpu.HBM)


def limit(mebibytes):
    return pltpu.CompilerParams(vmem_limit_bytes=mebibytes << 20)


def onchip(array):
    return pltpu.with_memory_space_constraint(array, pltpu.VMEM)


def next_side(across):
    odd = lax.rem(lax.axis_index("col"), 2)
    return odd if across else 1 - odd


def halo_kernel(across, occupied, tiles, out, sem):
    rows = tiles.shape[1]
    upward = next_side(across)
    copies = []
    spans = []
    start = 0
    for m in range(1, BAND + 1):
        count = BAND + 1 - m
        row = upward * (rows - m) + (1 - upward) * (m - 1)
        first = upward * m
        copies.append(
            pltpu.make_async_copy(
                tiles.at[:, row, pl.ds(first, count)],
                out.at[:, pl.ds(start, count)],
                sem.at[m - 1],
            )
        )
        spans.append((start, count, row, first))
        start += count
    for copy in copies:
        copy.start()
    for copy in copies:
        copy.wait()
    for start, count, row, first in spans:
        for step in range(count):
            d = first + step
            dropped = (d > 0) & jnp.logical_not(keep(occupied, row, jnp.maximum(d, 1)))

            @pl.when(dropped)
            def _():
                out[:, start + step] = jnp.zeros_like(out[:, start + step])


def halo_tiles(across, occupied, tiles):
    parts, _, _, height, width = tiles.shape
    return pl.pallas_call(
        functools.partial(halo_kernel, across),
        out_shape=pltpu.VMEM((parts, len(BELOW), height, width), tiles.dtype),
        in_specs=[SCALARS, OFFCHIP],
        out_specs=ONCHIP,
        scratch_shapes=[pltpu.SemaphoreType.DMA((BAND,))],
        compiler_params=limit(4),
    )(occupied, offchip(tiles))


def local_kernel(occupied, tiles, out, partial, strips, sem):
    parts, rows, _, height, _ = tiles.shape
    waiting = partial_tiles(rows)

    def block(row, d):
        return strips.at[row, :, :, pl.ds((BAND + d) * BLOCK, BLOCK)]

    def load(row, d):
        return pltpu.make_async_copy(tiles.at[:, row, d], block(row, d), sem.at[row, d])

    def get(row, d):
        return block(row, d)[...].reshape(BLOCK, BLOCK)

    def put(row, d, value):
        block(row, d)[...] = value.reshape(parts, height, BLOCK)

    for row in range(rows):
        for d in range(BAND + 1):
            load(row, d).start()

    def arrive(row):
        for d in range(BAND + 1):
            load(row, d).wait()
            if d > 0:

                @pl.when(jnp.logical_not(keep(occupied, row, d)))
                def _():
                    put(row, d, jnp.zeros((BLOCK, BLOCK), jnp.bfloat16))

    def prepare(j):
        if j < rows:
            arrive(j)
            put(j, 0, symmetric(get(j, 0)))
        for m in range(1, BAND + 1):
            if 0 <= j - m < rows:
                put(j, -m, get(j - m, m).T)

    for j in range(BAND):
        prepare(j)
    for i in range(rows):
        prepare(i + BAND)
        for e in range(BAND + 1):
            j = i + e
            first = max(0, j - BAND)
            last = i + BAND if j < rows else rows - 1
            depth = (last + 1 - first) * BLOCK
            rows_i = strips[i, :, :, pl.ds((first - i + BAND) * BLOCK, depth)]
            rows_j = strips[j, :, :, pl.ds((first - j + BAND) * BLOCK, depth)]
            summed = times_transposed(rows_i.reshape(BLOCK, depth), rows_j.reshape(BLOCK, depth))
            if (i, e) in waiting:
                partial[waiting.index((i, e))] = summed
            else:
                if e > 0:
                    summed = jnp.where(keep(occupied, i, e), summed, 0.0)
                out[:, i, e] = summed.astype(jnp.bfloat16).reshape(parts, height, BLOCK)


def square_local(occupied, tiles):
    parts, rows, width, height, _ = tiles.shape
    count = len(partial_tiles(rows))
    return pl.pallas_call(
        local_kernel,
        out_shape=(
            pltpu.VMEM(tiles.shape, jnp.bfloat16),
            pltpu.VMEM((count, BLOCK, BLOCK), jnp.float32),
        ),
        in_specs=[SCALARS, OFFCHIP],
        out_specs=(ONCHIP, ONCHIP),
        scratch_shapes=[
            pltpu.VMEM((rows + BAND, parts, height, LANES), jnp.bfloat16),
            pltpu.SemaphoreType.DMA((rows, width)),
        ],
        compiler_params=limit(30),
    )(occupied, offchip(tiles))


def border_kernel(across, occupied, sent, received, partial, _, out):
    parts, rows, _, height, _ = out.shape
    waiting = partial_tiles(rows)
    upward = next_side(across)

    def get(ref, slot):
        return ref[:, slot].reshape(BLOCK, BLOCK)

    def finish(i, e, summed):
        summed = partial[waiting.index((i, e))] + summed
        if e > 0:
            summed = jnp.where(keep(occupied, i, e), summed, 0.0)
        out[:, i, e] = summed.astype(jnp.bfloat16).reshape(parts, height, BLOCK)

    @pl.when(upward == 0)
    def _():
        lower = {
            j: jnp.concatenate(
                [get(received, BELOW.index((m, j + m))).T for m in range(BAND - j, 0, -1)],
                axis=1,
            )
            for j in range(BAND)
        }
        for j in range(BAND):
            depth = (BAND - j) * BLOCK
            for i in range(j + 1):
                rows_i = lower[i][:, lower[i].shape[1] - depth :]
                finish(i, j - i, times_transposed(rows_i, lower[j]))

    @pl.when(upward == 1)
    def _():
        def corner(a, b):
            if a == b:
                return symmetric(get(received, ABOVE.index((a, 0))))
            if a < b:
                return get(received, ABOVE.index((a, b - a)))
            return get(received, ABOVE.index((b, a - b))).T

        square = [
            jnp.concatenate([corner(a, b) for b in range(BAND)], axis=1) for a in range(BAND)
        ]
        for i in range(rows - BAND, rows):
            reach = i + BAND + 1 - rows
            rows_i = jnp.concatenate(
                [get(sent, BELOW.index((rows - i, rows + b - i))) for b in range(reach)], axis=1
            )
            for a in range(reach):
                finish(i, rows + a - i, times_transposed(rows_i, square[a][:, : reach * BLOCK]))


def square_border(across, occupied, sent, received, partial, product):
    return pl.pallas_call(
        functools.partial(border_kernel, across),
        out_shape=pltpu.VMEM(product.shape, product.dtype),
        in_specs=[SCALARS] + [ONCHIP] * 4,
        out_specs=ONCHIP,
        input_output_aliases={4: 0},
        compiler_params=limit(20),
    )(occupied, *(onchip(a) for a in (sent, received, partial, product)))


def swaps(firsts):
    return [pair for p in firsts for pair in ((p, p + 1), (p + 1, p))]


def shards(upper_tiles, occupied):
    parts = lax.axis_size("col")
    count = lax.axis_size("row") * parts
    rows = occupied.shape[0]
    tiles = upper_tiles.reshape((parts, rows) + upper_tiles.shape[1:])
    tiles = lax.all_to_all(tiles, "col", 0, 0, tiled=True)
    tiles, occupied = lax.optimization_barrier((tiles, occupied))
    sent_across = halo_tiles(True, occupied, tiles)
    across = lax.ppermute(sent_across, AXES, swaps(range(1, count - 1, 2)))
    sent_beside = halo_tiles(False, occupied, tiles)
    beside = lax.ppermute(sent_beside, AXES, swaps(range(0, count, 2)))
    product, partial = square_local(occupied, tiles)
    product = square_border(False, occupied, sent_beside, beside, partial, product)
    product = square_border(True, occupied, sent_across, across, partial, product)
    product = lax.all_to_all(product, "col", 0, 0, tiled=True)
    return product.reshape(upper_tiles.shape)


def solution(mesh):
    return jax.shard_map(
        shards,
        mesh=mesh,
        in_specs=(P("row", None, "col", None), P(("row", "col"), None)),
        out_specs=P("row", None, "col", None),
        check_vma=False,
    )
```

```python
import functools

import jax
import jax.numpy as jnp
from jax import lax
from jax.experimental import pallas as pl
from jax.experimental.pallas import tpu as pltpu
from jax.sharding import PartitionSpec as P


AXES = ("row", "col")
BLOCK = 256
BAND = 4
LANES = (2 * BAND + 1) * BLOCK
BELOW = [(m, d) for m in range(1, BAND + 1) for d in range(m, BAND + 1)]
ABOVE = [(m, d) for m in range(BAND) for d in range(BAND - m)]

SCALARS = pl.BlockSpec(memory_space=pltpu.SMEM)
ONCHIP = pl.BlockSpec(memory_space=pltpu.VMEM)


def partial_tiles(rows):
    return [
        (i, e) for i in range(rows) for e in range(BAND + 1) if i + e < BAND or i + e >= rows
    ]


def keep(occupied, row, d):
    rows = occupied.shape[1]
    here = lax.axis_index("row") * lax.axis_size("col") + lax.axis_index("col")
    there = lax.axis_size("row") * lax.axis_size("col")
    return (occupied[d - 1, row] == 1) & (here * rows + row + d < there * rows)


def times_transposed(left, right):
    return lax.dot_general(
        left, right, (((1,), (1,)), ((), ())), preferred_element_type=jnp.float32
    )


def symmetric(raw):
    both = raw.astype(jnp.float32) + raw.T.astype(jnp.float32)
    return (0.5 * both).astype(jnp.bfloat16)


def limit(mebibytes):
    return pltpu.CompilerParams(vmem_limit_bytes=mebibytes << 20)


def onchip(array):
    return pltpu.with_memory_space_constraint(array, pltpu.VMEM)


def next_side(across):
    odd = lax.rem(lax.axis_index("col"), 2)
    return odd if across else 1 - odd


def kept_tile(occupied, tiles, row, d):
    tile = tiles[:, row, d]
    return jnp.where(keep(occupied, row, d), tile, jnp.zeros_like(tile))


def halo_kernel(occupied, tiles, across, beside, _):
    rows = tiles.shape[1]
    odd = next_side(True)

    def gather(to_next, to_last):
        for slot, (m, d) in enumerate(BELOW):
            to_next[:, slot] = kept_tile(occupied, tiles, rows - m, d)
        for slot, (m, d) in enumerate(ABOVE):
            to_last[:, slot] = kept_tile(occupied, tiles, m, d) if d else tiles[:, m, d]

    @pl.when(odd == 1)
    def _():
        gather(across, beside)

    @pl.when(odd == 0)
    def _():
        gather(beside, across)


def halo_tiles(occupied, tiles):
    parts, _, _, height, width = tiles.shape
    halo = pltpu.VMEM((parts, len(BELOW), height, width), tiles.dtype)
    return pl.pallas_call(
        halo_kernel,
        out_shape=(halo, halo, pltpu.VMEM(tiles.shape, tiles.dtype)),
        in_specs=[SCALARS, ONCHIP],
        out_specs=(ONCHIP,) * 3,
        input_output_aliases={1: 2},
        compiler_params=limit(2),
    )(occupied, onchip(tiles))


def local_kernel(occupied, tiles, out, partial, strips):
    parts, rows, _, height, _ = tiles.shape
    waiting = partial_tiles(rows)

    def block(row, d):
        return strips.at[row, :, :, pl.ds((BAND + d) * BLOCK, BLOCK)]

    def put(row, d, value):
        block(row, d)[...] = value.reshape(parts, height, BLOCK)

    def prepare(j):
        if j < rows:
            put(j, 0, symmetric(tiles[:, j, 0].reshape(BLOCK, BLOCK)))
            for d in range(1, BAND + 1):
                put(j, d, kept_tile(occupied, tiles, j, d))
        for m in range(1, BAND + 1):
            if 0 <= j - m < rows:
                put(j, -m, block(j - m, m)[...].reshape(BLOCK, BLOCK).T)

    for j in range(BAND):
        prepare(j)
    for i in range(rows):
        prepare(i + BAND)
        for e in range(BAND + 1):
            j = i + e
            first = max(0, j - BAND)
            last = i + BAND if j < rows else rows - 1
            depth = (last + 1 - first) * BLOCK
            rows_i = strips[i, :, :, pl.ds((first - i + BAND) * BLOCK, depth)]
            rows_j = strips[j, :, :, pl.ds((first - j + BAND) * BLOCK, depth)]
            summed = times_transposed(rows_i.reshape(BLOCK, depth), rows_j.reshape(BLOCK, depth))
            if (i, e) in waiting:
                partial[waiting.index((i, e))] = summed
            else:
                if e > 0:
                    summed = jnp.where(keep(occupied, i, e), summed, 0.0)
                out[:, i, e] = summed.astype(jnp.bfloat16).reshape(parts, height, BLOCK)


def square_local(occupied, tiles):
    parts, rows, _, height, _ = tiles.shape
    count = len(partial_tiles(rows))
    return pl.pallas_call(
        local_kernel,
        out_shape=(
            pltpu.VMEM(tiles.shape, jnp.bfloat16),
            pltpu.VMEM((count, BLOCK, BLOCK), jnp.float32),
        ),
        in_specs=[SCALARS, ONCHIP],
        out_specs=(ONCHIP, ONCHIP),
        scratch_shapes=[
            pltpu.VMEM((rows + BAND, parts, height, LANES), jnp.bfloat16),
        ],
        compiler_params=limit(18),
    )(occupied, onchip(tiles))


def border_kernel(across, occupied, sent, received, partial, _, out):
    parts, rows, _, height, _ = out.shape
    waiting = partial_tiles(rows)
    upward = next_side(across)

    def get(ref, slot):
        return ref[:, slot].reshape(BLOCK, BLOCK)

    def finish(i, e, summed):
        summed = partial[waiting.index((i, e))] + summed
        if e > 0:
            summed = jnp.where(keep(occupied, i, e), summed, 0.0)
        out[:, i, e] = summed.astype(jnp.bfloat16).reshape(parts, height, BLOCK)

    @pl.when(upward == 0)
    def _():
        lower = {
            j: jnp.concatenate(
                [get(received, BELOW.index((m, j + m))).T for m in range(BAND - j, 0, -1)],
                axis=1,
            )
            for j in range(BAND)
        }
        for j in range(BAND):
            depth = (BAND - j) * BLOCK
            for i in range(j + 1):
                rows_i = lower[i][:, lower[i].shape[1] - depth :]
                finish(i, j - i, times_transposed(rows_i, lower[j]))

    @pl.when(upward == 1)
    def _():
        def corner(a, b):
            if a == b:
                return symmetric(get(received, ABOVE.index((a, 0))))
            if a < b:
                return get(received, ABOVE.index((a, b - a)))
            return get(received, ABOVE.index((b, a - b))).T

        square = [
            jnp.concatenate([corner(a, b) for b in range(BAND)], axis=1) for a in range(BAND)
        ]
        for i in range(rows - BAND, rows):
            reach = i + BAND + 1 - rows
            rows_i = jnp.concatenate(
                [get(sent, BELOW.index((rows - i, rows + b - i))) for b in range(reach)], axis=1
            )
            for a in range(reach):
                finish(i, rows + a - i, times_transposed(rows_i, square[a][:, : reach * BLOCK]))


def square_border(across, occupied, sent, received, partial, product):
    return pl.pallas_call(
        functools.partial(border_kernel, across),
        out_shape=pltpu.VMEM(product.shape, product.dtype),
        in_specs=[SCALARS] + [ONCHIP] * 4,
        out_specs=ONCHIP,
        input_output_aliases={4: 0},
        compiler_params=limit(8),
    )(occupied, *(onchip(a) for a in (sent, received, partial, product)))


def swaps(firsts):
    return [pair for p in firsts for pair in ((p, p + 1), (p + 1, p))]


def shards(upper_tiles, occupied):
    parts = lax.axis_size("col")
    count = lax.axis_size("row") * parts
    rows = occupied.shape[0]
    tiles = upper_tiles.reshape((parts, rows) + upper_tiles.shape[1:])
    tiles = lax.all_to_all(tiles, "col", 0, 0, tiled=True)
    occupied = occupied.T
    sent_across, sent_beside, tiles = halo_tiles(occupied, tiles)
    across = lax.ppermute(sent_across, AXES, swaps(range(1, count - 1, 2)))
    beside = lax.ppermute(sent_beside, AXES, swaps(range(0, count, 2)))
    product, partial = square_local(occupied, tiles)
    product = square_border(False, occupied, sent_beside, beside, partial, product)
    product = square_border(True, occupied, sent_across, across, partial, product)
    product = lax.all_to_all(product, "col", 0, 0, tiled=True)
    return product.reshape(upper_tiles.shape)


def solution(mesh):
    return jax.shard_map(
        shards,
        mesh=mesh,
        in_specs=(P("row", None, "col", None), P(("row", "col"), None)),
        out_specs=P("row", None, "col", None),
        check_vma=False,
    )
```

```python
import functools

import jax
import jax.numpy as jnp
from jax import lax
from jax.experimental import pallas as pl
from jax.experimental.pallas import tpu as pltpu
from jax.sharding import PartitionSpec as P


AXES = ("row", "col")
BLOCK = 256
BAND = 4
LANES = (2 * BAND + 1) * BLOCK
BELOW = [(m, d) for m in range(1, BAND + 1) for d in range(m, BAND + 1)]
ABOVE = [(m, d) for m in range(BAND) for d in range(BAND - m)]

SCALARS = pl.BlockSpec(memory_space=pltpu.SMEM)
ONCHIP = pl.BlockSpec(memory_space=pltpu.VMEM)


def partial_tiles(rows):
    return [
        (i, e) for i in range(rows) for e in range(BAND + 1) if i + e < BAND or i + e >= rows
    ]


def chain(parts):
    half = parts // 2
    return list(range(half)) + [half + parts - 2 - c + 2 * (c % 2) for c in range(half, parts)]


def place(array):
    pieces = []
    for part in chain(array.shape[0]):
        if pieces and part == pieces[-1][1]:
            pieces[-1][1] = part + 1
        else:
            pieces.append([part, part + 1])
    return jnp.concatenate([array[first:last] for first, last in pieces], axis=0)


def seat():
    parts = lax.axis_size("col")
    half = parts // 2
    col = lax.axis_index("col")
    late = col // half
    mirrored = half + parts - 2 - col + 2 * lax.rem(col, 2)
    return lax.axis_index("row") * parts + (1 - late) * col + late * mirrored


def keep(occupied, row, d, away=0):
    rows = occupied.shape[1]
    total = lax.axis_size("row") * lax.axis_size("col") * rows
    return (occupied[d - 1, row] == 1) & ((seat() + away) * rows + row + d < total)


def times_transposed(left, right):
    return lax.dot_general(
        left, right, (((1,), (1,)), ((), ())), preferred_element_type=jnp.float32
    )


def symmetric(raw):
    both = raw.astype(jnp.float32) + raw.T.astype(jnp.float32)
    return (0.5 * both).astype(jnp.bfloat16)


def limit(mebibytes):
    return pltpu.CompilerParams(vmem_limit_bytes=mebibytes << 20)


def onchip(array):
    return pltpu.with_memory_space_constraint(array, pltpu.VMEM)


def next_side(across):
    odd = lax.rem(lax.axis_index("col"), 2)
    return odd if across else 1 - odd


def kept_tile(occupied, tile, row, d, away=0):
    return jnp.where(keep(occupied, row, d, away), tile, jnp.zeros_like(tile))


def halo_kernel(tiles, across, beside, _):
    rows = tiles.shape[1]
    odd = next_side(True)

    def gather(to_next, to_last):
        for slot, (m, d) in enumerate(BELOW):
            to_next[:, slot] = place(tiles[:, rows - m, d])
        for slot, (m, d) in enumerate(ABOVE):
            to_last[:, slot] = place(tiles[:, m, d])

    @pl.when(odd == 1)
    def _():
        gather(across, beside)

    @pl.when(odd == 0)
    def _():
        gather(beside, across)


def halo_tiles(tiles):
    parts, _, _, height, width = tiles.shape
    halo = pltpu.VMEM((parts, len(BELOW), height, width), tiles.dtype)
    return pl.pallas_call(
        halo_kernel,
        out_shape=(halo, halo, pltpu.VMEM(tiles.shape, tiles.dtype)),
        in_specs=[ONCHIP],
        out_specs=(ONCHIP,) * 3,
        input_output_aliases={0: 2},
        compiler_params=limit(2),
    )(onchip(tiles))


def local_kernel(occupied, tiles, out, partial, strips):
    parts, rows, _, height, _ = tiles.shape
    waiting = partial_tiles(rows)

    def block(row, d):
        return strips.at[row, :, :, pl.ds((BAND + d) * BLOCK, BLOCK)]

    def put(row, d, value):
        block(row, d)[...] = value.reshape(parts, height, BLOCK)

    def prepare(j):
        if j < rows:
            put(j, 0, symmetric(place(tiles[:, j, 0]).reshape(BLOCK, BLOCK)))
            for d in range(1, BAND + 1):
                put(j, d, kept_tile(occupied, place(tiles[:, j, d]), j, d))
        for m in range(1, BAND + 1):
            if 0 <= j - m < rows:
                put(j, -m, block(j - m, m)[...].reshape(BLOCK, BLOCK).T)

    for j in range(BAND):
        prepare(j)
    for i in range(rows):
        prepare(i + BAND)
        for e in range(BAND + 1):
            j = i + e
            first = max(0, j - BAND)
            last = i + BAND if j < rows else rows - 1
            depth = (last + 1 - first) * BLOCK
            rows_i = strips[i, :, :, pl.ds((first - i + BAND) * BLOCK, depth)]
            rows_j = strips[j, :, :, pl.ds((first - j + BAND) * BLOCK, depth)]
            summed = times_transposed(rows_i.reshape(BLOCK, depth), rows_j.reshape(BLOCK, depth))
            if (i, e) in waiting:
                partial[waiting.index((i, e))] = summed
            else:
                if e > 0:
                    summed = jnp.where(keep(occupied, i, e), summed, 0.0)
                out[:, i, e] = place(summed.astype(jnp.bfloat16).reshape(parts, height, BLOCK))


def square_local(occupied, tiles):
    parts, rows, _, height, _ = tiles.shape
    count = len(partial_tiles(rows))
    return pl.pallas_call(
        local_kernel,
        out_shape=(
            pltpu.VMEM(tiles.shape, jnp.bfloat16),
            pltpu.VMEM((count, BLOCK, BLOCK), jnp.float32),
        ),
        in_specs=[SCALARS, ONCHIP],
        out_specs=(ONCHIP, ONCHIP),
        scratch_shapes=[
            pltpu.VMEM((rows + BAND, parts, height, LANES), jnp.bfloat16),
        ],
        compiler_params=limit(18),
    )(occupied, onchip(tiles))


def border_kernel(across, occupied, theirs, sent, received, partial, _, out):
    parts, rows, _, height, _ = out.shape
    waiting = partial_tiles(rows)
    upward = next_side(across)

    def below(m, d):
        tile = kept_tile(theirs, received[:, BELOW.index((m, d))], rows - m, d, -1)
        return tile.reshape(BLOCK, BLOCK)

    def above(m, d):
        tile = received[:, ABOVE.index((m, d))]
        if d:
            tile = kept_tile(theirs, tile, m, d, 1)
        return tile.reshape(BLOCK, BLOCK)

    def own(m, d):
        tile = kept_tile(occupied, sent[:, BELOW.index((m, d))], rows - m, d)
        return tile.reshape(BLOCK, BLOCK)

    def finish(i, e, summed):
        summed = partial[waiting.index((i, e))] + summed
        if e > 0:
            summed = jnp.where(keep(occupied, i, e), summed, 0.0)
        out[:, i, e] = place(summed.astype(jnp.bfloat16).reshape(parts, height, BLOCK))

    @pl.when(upward == 0)
    def _():
        lower = {
            j: jnp.concatenate(
                [below(m, j + m).T for m in range(BAND - j, 0, -1)],
                axis=1,
            )
            for j in range(BAND)
        }
        for j in range(BAND):
            depth = (BAND - j) * BLOCK
            for i in range(j + 1):
                rows_i = lower[i][:, lower[i].shape[1] - depth :]
                finish(i, j - i, times_transposed(rows_i, lower[j]))

    @pl.when(upward == 1)
    def _():
        def corner(a, b):
            if a == b:
                return symmetric(above(a, 0))
            if a < b:
                return above(a, b - a)
            return above(b, a - b).T

        square = [
            jnp.concatenate([corner(a, b) for b in range(BAND)], axis=1) for a in range(BAND)
        ]
        for i in range(rows - BAND, rows):
            reach = i + BAND + 1 - rows
            rows_i = jnp.concatenate(
                [own(rows - i, rows + b - i) for b in range(reach)], axis=1
            )
            for a in range(reach):
                finish(i, rows + a - i, times_transposed(rows_i, square[a][:, : reach * BLOCK]))


def square_border(across, occupied, theirs, sent, received, partial, product):
    return pl.pallas_call(
        functools.partial(border_kernel, across),
        out_shape=pltpu.VMEM(product.shape, product.dtype),
        in_specs=[SCALARS] * 2 + [ONCHIP] * 4,
        out_specs=ONCHIP,
        input_output_aliases={5: 0},
        compiler_params=limit(8),
    )(occupied, theirs, *(onchip(a) for a in (sent, received, partial, product)))


def exchange(array):
    parts = lax.axis_size("col")
    return lax.all_to_all(array, "col", 0, 0, axis_index_groups=[chain(parts)], tiled=True)


def shards(upper_tiles, occupied):
    parts = lax.axis_size("col")
    count = lax.axis_size("row") * parts
    rows = occupied.shape[0]
    device = [p // parts * parts + chain(parts)[p % parts] for p in range(count)]
    facing = [(p, p + 1 if p % 2 else p - 1) for p in range(1, count - 1)]
    paired = [(p, p ^ 1) for p in range(count)]

    def swap(array, places):
        return lax.ppermute(array, AXES, [(device[p], device[q]) for p, q in places])

    tiles = exchange(upper_tiles.reshape((parts, rows) + upper_tiles.shape[1:]))
    sent_across, sent_beside, tiles = halo_tiles(tiles)
    across = swap(sent_across, facing)
    beside = swap(sent_beside, paired)
    occupied = occupied.T
    own = lax.ppermute(occupied, AXES, [(p, device[p]) for p in range(count)])
    near = lax.ppermute(occupied, AXES, [(p, device[q]) for p, q in paired])
    far = lax.ppermute(occupied, AXES, [(p, device[q]) for p, q in facing])
    product, partial = square_local(own, tiles)
    product = square_border(False, own, near, sent_beside, beside, partial, product)
    product = square_border(True, own, far, sent_across, across, partial, product)
    return exchange(product).reshape(upper_tiles.shape)


def solution(mesh):
    return jax.shard_map(
        shards,
        mesh=mesh,
        in_specs=(P("row", None, "col", None), P(("row", "col"), None)),
        out_specs=P("row", None, "col", None),
        check_vma=False,
    )
```

```python
import functools

import jax
import jax.numpy as jnp
from jax import lax
from jax.experimental import pallas as pl
from jax.experimental.pallas import tpu as pltpu
from jax.sharding import PartitionSpec as P


AXES = ("row", "col")
BLOCK = 256
BAND = 4
LANES = (2 * BAND + 1) * BLOCK
BELOW = [(m, d) for m in range(1, BAND + 1) for d in range(m, BAND + 1)]
ABOVE = [(m, d) for m in range(BAND) for d in range(BAND - m)]

SCALARS = pl.BlockSpec(memory_space=pltpu.SMEM)
ONCHIP = pl.BlockSpec(memory_space=pltpu.VMEM)


def partial_tiles(rows):
    return [
        (i, e) for i in range(rows) for e in range(BAND + 1) if i + e < BAND or i + e >= rows
    ]


def keep(occupied, row, d):
    rows = occupied.shape[1]
    here = lax.axis_index("row") * lax.axis_size("col") + lax.axis_index("col")
    there = lax.axis_size("row") * lax.axis_size("col")
    return (occupied[d - 1, row] == 1) & (here * rows + row + d < there * rows)


def times_transposed(left, right):
    return lax.dot_general(
        left, right, (((1,), (1,)), ((), ())), preferred_element_type=jnp.float32
    )


def symmetric(raw):
    both = raw.astype(jnp.float32) + raw.T.astype(jnp.float32)
    return (0.5 * both).astype(jnp.bfloat16)


def limit(mebibytes):
    return pltpu.CompilerParams(vmem_limit_bytes=mebibytes << 20)


def onchip(array):
    return pltpu.with_memory_space_constraint(array, pltpu.VMEM)


def next_side(across):
    odd = lax.rem(lax.axis_index("col"), 2)
    return odd if across else 1 - odd


def pattern(occupied):
    rows = occupied.shape[1]
    here = lax.axis_index("row") * lax.axis_size("col") + lax.axis_index("col")
    there = lax.axis_size("row") * lax.axis_size("col")
    row = lax.broadcasted_iota(jnp.int32, occupied.shape, 1)
    d = lax.broadcasted_iota(jnp.int32, occupied.shape, 0) + 1
    inside = row + d < (there - here) * rows
    return jnp.where((occupied[...] == 1) & inside, 1.0, 0.0)


def spread(mask, row, d, height):
    return jnp.broadcast_to(mask[d - 1 : d, row : row + 1], (height, BLOCK))


def kept_tile(occupied, tiles, row, d):
    tile = tiles[:, row, d]
    return jnp.where(keep(occupied, row, d), tile, jnp.zeros_like(tile))


def halo_kernel(occupied, tiles, across, beside, _):
    rows = tiles.shape[1]
    odd = next_side(True)

    mask = pattern(occupied)

    def masked(row, d):
        scale = spread(mask, row, d, tiles.shape[3]).astype(tiles.dtype)
        return tiles[:, row, d] * scale[None]

    def gather(to_next, to_last):
        for slot, (m, d) in enumerate(BELOW):
            to_next[:, slot] = masked(rows - m, d)
        for slot, (m, d) in enumerate(ABOVE):
            to_last[:, slot] = masked(m, d) if d else tiles[:, m, d]

    @pl.when(odd == 1)
    def _():
        gather(across, beside)

    @pl.when(odd == 0)
    def _():
        gather(beside, across)


def halo_tiles(occupied, tiles):
    parts, _, _, height, width = tiles.shape
    halo = pltpu.VMEM((parts, len(BELOW), height, width), tiles.dtype)
    return pl.pallas_call(
        halo_kernel,
        out_shape=(halo, halo, pltpu.VMEM(tiles.shape, tiles.dtype)),
        in_specs=[ONCHIP, ONCHIP],
        out_specs=(ONCHIP,) * 3,
        input_output_aliases={1: 2},
        compiler_params=limit(2),
    )(occupied, onchip(tiles))


def local_kernel(occupied, tiles, out, partial, strips):
    parts, rows, _, height, _ = tiles.shape
    waiting = partial_tiles(rows)

    def block(row, d):
        return strips.at[row, :, :, pl.ds((BAND + d) * BLOCK, BLOCK)]

    def put(row, d, value):
        block(row, d)[...] = value.reshape(parts, height, BLOCK)

    def prepare(j):
        if j < rows:
            put(j, 0, symmetric(tiles[:, j, 0].reshape(BLOCK, BLOCK)))
            for d in range(1, BAND + 1):
                put(j, d, kept_tile(occupied, tiles, j, d))
        for m in range(1, BAND + 1):
            if 0 <= j - m < rows:
                put(j, -m, block(j - m, m)[...].reshape(BLOCK, BLOCK).T)

    for j in range(BAND):
        prepare(j)
    for i in range(rows):
        prepare(i + BAND)
        for e in range(BAND + 1):
            j = i + e
            first = max(0, j - BAND)
            last = i + BAND if j < rows else rows - 1
            depth = (last + 1 - first) * BLOCK
            rows_i = strips[i, :, :, pl.ds((first - i + BAND) * BLOCK, depth)]
            rows_j = strips[j, :, :, pl.ds((first - j + BAND) * BLOCK, depth)]
            summed = times_transposed(rows_i.reshape(BLOCK, depth), rows_j.reshape(BLOCK, depth))
            if (i, e) in waiting:
                partial[waiting.index((i, e))] = summed
            else:
                if e > 0:
                    summed = jnp.where(keep(occupied, i, e), summed, 0.0)
                out[:, i, e] = summed.astype(jnp.bfloat16).reshape(parts, height, BLOCK)


def square_local(occupied, tiles):
    parts, rows, _, height, _ = tiles.shape
    count = len(partial_tiles(rows))
    return pl.pallas_call(
        local_kernel,
        out_shape=(
            pltpu.VMEM(tiles.shape, jnp.bfloat16),
            pltpu.VMEM((count, BLOCK, BLOCK), jnp.float32),
        ),
        in_specs=[SCALARS, ONCHIP],
        out_specs=(ONCHIP, ONCHIP),
        scratch_shapes=[
            pltpu.VMEM((rows + BAND, parts, height, LANES), jnp.bfloat16),
        ],
        compiler_params=limit(18),
    )(occupied, onchip(tiles))


def border_kernel(across, occupied, sent, received, partial, _, out):
    parts, rows, _, height, _ = out.shape
    waiting = partial_tiles(rows)
    upward = next_side(across)
    mask = pattern(occupied)

    def get(ref, slot):
        return ref[:, slot].reshape(BLOCK, BLOCK)

    def finish(i, e, summed):
        summed = partial[waiting.index((i, e))] + summed
        if e > 0:
            summed = jnp.where(spread(mask, i, e, BLOCK) > 0.5, summed, 0.0)
        out[:, i, e] = summed.astype(jnp.bfloat16).reshape(parts, height, BLOCK)

    @pl.when(upward == 0)
    def _():
        lower = {
            j: jnp.concatenate(
                [get(received, BELOW.index((m, j + m))).T for m in range(BAND - j, 0, -1)],
                axis=1,
            )
            for j in range(BAND)
        }
        for j in range(BAND):
            depth = (BAND - j) * BLOCK
            for i in range(j + 1):
                rows_i = lower[i][:, lower[i].shape[1] - depth :]
                finish(i, j - i, times_transposed(rows_i, lower[j]))

    @pl.when(upward == 1)
    def _():
        def corner(a, b):
            if a == b:
                return symmetric(get(received, ABOVE.index((a, 0))))
            if a < b:
                return get(received, ABOVE.index((a, b - a)))
            return get(received, ABOVE.index((b, a - b))).T

        square = [
            jnp.concatenate([corner(a, b) for b in range(BAND)], axis=1) for a in range(BAND)
        ]
        for i in range(rows - BAND, rows):
            reach = i + BAND + 1 - rows
            rows_i = jnp.concatenate(
                [get(sent, BELOW.index((rows - i, rows + b - i))) for b in range(reach)], axis=1
            )
            for a in range(reach):
                finish(i, rows + a - i, times_transposed(rows_i, square[a][:, : reach * BLOCK]))


def square_border(across, occupied, sent, received, partial, product):
    return pl.pallas_call(
        functools.partial(border_kernel, across),
        out_shape=pltpu.VMEM(product.shape, product.dtype),
        in_specs=[ONCHIP] * 5,
        out_specs=ONCHIP,
        input_output_aliases={4: 0},
        compiler_params=limit(8),
    )(occupied, *(onchip(a) for a in (sent, received, partial, product)))


def swaps(firsts):
    return [pair for p in firsts for pair in ((p, p + 1), (p + 1, p))]


def shards(upper_tiles, occupied):
    parts = lax.axis_size("col")
    count = lax.axis_size("row") * parts
    rows = occupied.shape[0]
    tiles = upper_tiles.reshape((parts, rows) + upper_tiles.shape[1:])
    tiles = lax.all_to_all(tiles, "col", 0, 0, tiled=True)
    occupied = occupied.T
    sent_across, sent_beside, tiles = halo_tiles(occupied, tiles)
    across = lax.ppermute(sent_across, AXES, swaps(range(1, count - 1, 2)))
    beside = lax.ppermute(sent_beside, AXES, swaps(range(0, count, 2)))
    product, partial = square_local(occupied, tiles)
    product = square_border(False, occupied, sent_beside, beside, partial, product)
    product = square_border(True, occupied, sent_across, across, partial, product)
    product = lax.all_to_all(product, "col", 0, 0, tiled=True)
    return product.reshape(upper_tiles.shape)


def solution(mesh):
    return jax.shard_map(
        shards,
        mesh=mesh,
        in_specs=(P("row", None, "col", None), P(("row", "col"), None)),
        out_specs=P("row", None, "col", None),
        check_vma=False,
    )
```

```python
import functools

import jax
import jax.numpy as jnp
from jax import lax
from jax.experimental import pallas as pl
from jax.experimental.pallas import tpu as pltpu
from jax.sharding import PartitionSpec as P


AXES = ("row", "col")
BLOCK = 256
BAND = 4
LANES = (2 * BAND + 1) * BLOCK
BELOW = [(m, d) for m in range(1, BAND + 1) for d in range(m + 1, BAND + 1)]
SPLIT = len(BELOW)
BELOW += [(m, m) for m in range(1, BAND + 1)]
ABOVE = [(m, d) for m in range(BAND) for d in range(BAND - 1 - m)]
ABOVE += [(m, BAND - 1 - m) for m in range(BAND)]

SCALARS = pl.BlockSpec(memory_space=pltpu.SMEM)
ONCHIP = pl.BlockSpec(memory_space=pltpu.VMEM)


def partial_tiles(rows):
    return [
        (i, e) for i in range(rows) for e in range(BAND + 1) if i + e < BAND or i + e >= rows
    ]


def keep(occupied, row, d):
    rows = occupied.shape[1]
    here = lax.axis_index("row") * lax.axis_size("col") + lax.axis_index("col")
    there = lax.axis_size("row") * lax.axis_size("col")
    return (occupied[d - 1, row] == 1) & (here * rows + row + d < there * rows)


def times_transposed(left, right):
    return lax.dot_general(
        left, right, (((1,), (1,)), ((), ())), preferred_element_type=jnp.float32
    )


def symmetric(raw):
    both = raw.astype(jnp.float32) + raw.T.astype(jnp.float32)
    return (0.5 * both).astype(jnp.bfloat16)


def limit(mebibytes):
    return pltpu.CompilerParams(vmem_limit_bytes=mebibytes << 20)


def onchip(array):
    return pltpu.with_memory_space_constraint(array, pltpu.VMEM)


def next_side(across):
    odd = lax.rem(lax.axis_index("col"), 2)
    return odd if across else 1 - odd


def pattern(occupied):
    rows = occupied.shape[1]
    here = lax.axis_index("row") * lax.axis_size("col") + lax.axis_index("col")
    there = lax.axis_size("row") * lax.axis_size("col")
    row = lax.broadcasted_iota(jnp.int32, occupied.shape, 1)
    d = lax.broadcasted_iota(jnp.int32, occupied.shape, 0) + 1
    inside = row + d < (there - here) * rows
    return jnp.where((occupied[...] == 1) & inside, 1.0, 0.0)


def spread(mask, row, d, height):
    return jnp.broadcast_to(mask[d - 1 : d, row : row + 1], (height, BLOCK))


def kept_tile(occupied, tiles, row, d):
    tile = tiles[:, row, d]
    return jnp.where(keep(occupied, row, d), tile, jnp.zeros_like(tile))


def pick(refs, slot):
    if len(refs) == 1 or slot < SPLIT:
        return refs[0], slot
    return refs[1], slot - SPLIT


def halo_kernel(occupied, tiles, early, late, beside, _):
    rows = tiles.shape[1]
    odd = next_side(True)

    mask = pattern(occupied)

    def masked(row, d):
        scale = spread(mask, row, d, tiles.shape[3]).astype(tiles.dtype)
        return tiles[:, row, d] * scale[None]

    def gather(to_next, to_last):
        for slot, (m, d) in enumerate(BELOW):
            put(to_next, slot, masked(rows - m, d))
        for slot, (m, d) in enumerate(ABOVE):
            put(to_last, slot, masked(m, d) if d else tiles[:, m, d])

    def put(refs, slot, value):
        ref, at = pick(refs, slot)
        ref[:, at] = value

    @pl.when(odd == 1)
    def _():
        gather((early, late), (beside,))

    @pl.when(odd == 0)
    def _():
        gather((beside,), (early, late))


def halo_tiles(occupied, tiles):
    parts, _, _, height, width = tiles.shape
    early, late, whole = (
        pltpu.VMEM((parts, count, height, width), tiles.dtype)
        for count in (SPLIT, len(BELOW) - SPLIT, len(BELOW))
    )
    return pl.pallas_call(
        halo_kernel,
        out_shape=(early, late, whole, pltpu.VMEM(tiles.shape, tiles.dtype)),
        in_specs=[ONCHIP, ONCHIP],
        out_specs=(ONCHIP,) * 4,
        input_output_aliases={1: 3},
        compiler_params=limit(2),
    )(occupied, onchip(tiles))


def local_kernel(occupied, tiles, out, partial, strips):
    parts, rows, _, height, _ = tiles.shape
    waiting = partial_tiles(rows)

    def block(row, d):
        return strips.at[row, :, :, pl.ds((BAND + d) * BLOCK, BLOCK)]

    def put(row, d, value):
        block(row, d)[...] = value.reshape(parts, height, BLOCK)

    def prepare(j):
        if j < rows:
            put(j, 0, symmetric(tiles[:, j, 0].reshape(BLOCK, BLOCK)))
            for d in range(1, BAND + 1):
                put(j, d, kept_tile(occupied, tiles, j, d))
        for m in range(1, BAND + 1):
            if 0 <= j - m < rows:
                put(j, -m, block(j - m, m)[...].reshape(BLOCK, BLOCK).T)

    for j in range(BAND):
        prepare(j)
    for i in range(rows):
        prepare(i + BAND)
        for e in range(BAND + 1):
            j = i + e
            first = max(0, j - BAND)
            last = i + BAND if j < rows else rows - 1
            depth = (last + 1 - first) * BLOCK
            rows_i = strips[i, :, :, pl.ds((first - i + BAND) * BLOCK, depth)]
            rows_j = strips[j, :, :, pl.ds((first - j + BAND) * BLOCK, depth)]
            summed = times_transposed(rows_i.reshape(BLOCK, depth), rows_j.reshape(BLOCK, depth))
            if (i, e) in waiting:
                partial[waiting.index((i, e))] = summed
            else:
                if e > 0:
                    summed = jnp.where(keep(occupied, i, e), summed, 0.0)
                out[:, i, e] = summed.astype(jnp.bfloat16).reshape(parts, height, BLOCK)


def square_local(occupied, tiles):
    parts, rows, _, height, _ = tiles.shape
    count = len(partial_tiles(rows))
    return pl.pallas_call(
        local_kernel,
        out_shape=(
            pltpu.VMEM(tiles.shape, jnp.bfloat16),
            pltpu.VMEM((count, BLOCK, BLOCK), jnp.float32),
        ),
        in_specs=[SCALARS, ONCHIP],
        out_specs=(ONCHIP, ONCHIP),
        scratch_shapes=[
            pltpu.VMEM((rows + BAND, parts, height, LANES), jnp.bfloat16),
        ],
        compiler_params=limit(18),
    )(occupied, onchip(tiles))


def border_kernel(across, stages, pieces, occupied, *refs):
    sent, received = refs[: pieces[0]], refs[pieces[0] : sum(pieces)]
    partial, _, out = refs[sum(pieces) :]
    parts, rows, _, height, _ = out.shape
    waiting = partial_tiles(rows)
    upward = next_side(across)
    mask = pattern(occupied)

    def get(arrays, slot):
        ref, at = pick(arrays, slot)
        return ref[:, at].reshape(BLOCK, BLOCK)

    def finish(i, e, summed):
        summed = partial[waiting.index((i, e))] + summed
        if e > 0:
            summed = jnp.where(spread(mask, i, e, BLOCK) > 0.5, summed, 0.0)
        out[:, i, e] = summed.astype(jnp.bfloat16).reshape(parts, height, BLOCK)

    @pl.when(upward == 0)
    def _():
        lower = {
            j: jnp.concatenate(
                [get(received, BELOW.index((m, j + m))).T for m in range(BAND - j, 0, -1)],
                axis=1,
            )
            for j in range(0 if 1 in stages else 1, BAND)
        }
        for j in lower:
            depth = (BAND - j) * BLOCK
            for i in range(j + 1):
                if (0 if i else 1) not in stages:
                    continue
                rows_i = lower[i][:, lower[i].shape[1] - depth :]
                finish(i, j - i, times_transposed(rows_i, lower[j]))

    @pl.when(upward == 1)
    def _():
        def corner(a, b):
            if a == b:
                return symmetric(get(received, ABOVE.index((a, 0))))
            if a < b:
                return get(received, ABOVE.index((a, b - a)))
            return get(received, ABOVE.index((b, a - b))).T

        size = BAND if 1 in stages else BAND - 1
        square = [
            jnp.concatenate([corner(a, b) for b in range(size)], axis=1) for a in range(size)
        ]
        for i in range(rows - BAND, rows):
            if (1 if i == rows - 1 else 0) not in stages:
                continue
            reach = i + BAND + 1 - rows
            rows_i = jnp.concatenate(
                [get(sent, BELOW.index((rows - i, rows + b - i))) for b in range(reach)], axis=1
            )
            for a in range(reach):
                finish(i, rows + a - i, times_transposed(rows_i, square[a][:, : reach * BLOCK]))


def square_border(across, stages, occupied, sent, received, partial, product):
    return pl.pallas_call(
        functools.partial(border_kernel, across, stages, (len(sent), len(received))),
        out_shape=pltpu.VMEM(product.shape, product.dtype),
        in_specs=[ONCHIP] * (3 + len(sent) + len(received)),
        out_specs=ONCHIP,
        input_output_aliases={2 + len(sent) + len(received): 0},
        compiler_params=limit(8),
    )(occupied, *(onchip(a) for a in (*sent, *received, partial, product)))


def swaps(firsts):
    return [pair for p in firsts for pair in ((p, p + 1), (p + 1, p))]


def shards(upper_tiles, occupied):
    parts = lax.axis_size("col")
    count = lax.axis_size("row") * parts
    rows = occupied.shape[0]
    tiles = upper_tiles.reshape((parts, rows) + upper_tiles.shape[1:])
    tiles = lax.all_to_all(tiles, "col", 0, 0, tiled=True)
    occupied = occupied.T
    early, late, sent_beside, tiles = halo_tiles(occupied, tiles)
    facing = swaps(range(1, count - 1, 2))
    first = lax.ppermute(early, AXES, facing)
    second = lax.ppermute(late, AXES, facing)
    beside = lax.ppermute(sent_beside, AXES, swaps(range(0, count, 2)))
    sent = (early, late)
    product, partial = square_local(occupied, tiles)
    product = square_border(False, (0, 1), occupied, (sent_beside,), (beside,), partial, product)
    product = square_border(True, (0,), occupied, sent, (first,), partial, product)
    product = square_border(True, (1,), occupied, sent, (first, second), partial, product)
    product = lax.all_to_all(product, "col", 0, 0, tiled=True)
    return product.reshape(upper_tiles.shape)


def solution(mesh):
    return jax.shard_map(
        shards,
        mesh=mesh,
        in_specs=(P("row", None, "col", None), P(("row", "col"), None)),
        out_specs=P("row", None, "col", None),
        check_vma=False,
    )
```
